32 devices in a mesh: dp: 4 (over y, x), ctx: 8 (over z, core).
Axes of the slice: x: 2, y: 2, z: 4, core: 2. Of those that a mesh axis runs over, the one named last changes fastest.
Arguments:
- inputs: bfloat16 [4096, 960], P(('dp', 'ctx')), may hold values from -6 to 6
- cotangent: bfloat16 [4096, 960], P(('dp', 'ctx')), may hold values from -6 to 6
- w_query: bfloat16 [960, 960], P('dp', 'ctx'), may hold values from -1 to 1
- w_key: bfloat16 [960, 320], P('dp', 'ctx'), may hold values from -1 to 1
- w_value: bfloat16 [960, 320], P('dp', 'ctx'), may hold values from -0.1875 to 0.1875
- w_output: bfloat16 [960, 960], P('dp', 'ctx'), may hold values from -0.75 to 0.75
- w_gate: bfloat16 [960, 2560], P('dp', 'ctx'), may hold values from -0.1875 to 0.1875
- w_up: bfloat16 [960, 2560], P('dp', 'ctx'), may hold values from -0.1875 to 0.1875
- w_down: bfloat16 [2560, 960], P('dp', 'ctx'), may hold values from -0.125 to 0.125
- gain_attn: bfloat16 [960], P('ctx'), may hold values from 0.5 to 1.5
- gain_ffn: bfloat16 [960], P('ctx'), may hold values from 0.5 to 1.5
Outputs:
- out_act: bfloat16 [4096, 960], P(('dp', 'ctx'))
- grad_input: float32 [4096, 960], P(('dp', 'ctx'))
- grad_w_query: float32 [960, 960], P('dp', 'ctx')
- grad_w_key: float32 [960, 320], P('dp', 'ctx')
- grad_w_value: float32 [960, 320], P('dp', 'ctx')
- grad_w_output: float32 [960, 960], P('dp', 'ctx')
- grad_w_gate: float32 [960, 2560], P('dp', 'ctx')
- grad_w_up: float32 [960, 2560], P('dp', 'ctx')
- grad_w_down: float32 [2560, 960], P('dp', 'ctx')
- grad_gain_attn: float32 [960], P('ctx')
- grad_gain_ffn: float32 [960], P('ctx')
The draws below stay inside these ranges and needn't reach their ends.
All inputs are finite; a program needn't handle non-finite values.
Results may differ from the reference program's by a relative error of at most 0.028.
Values may be sent and summed in bfloat16 or wider, within the bound.
A program may use at most 128 MiB of HBM per device.

```python
import jax
import jax.numpy as jnp
from jax import lax

D = 960
HEADS = 15
KV_HEADS = 5
HEAD_DIM = 64
FF = 2560
TOK_DEV = 128
SEQS = 4
LENGTH = 1024
TOKENS = 4096


def draw_inputs(key, part):
    input_key = jax.random.fold_in(key, 11)
    normal_key = jax.random.fold_in(input_key, 0)
    drawn_draw = jax.random.truncated_normal(normal_key, -6.0, 6.0, (TOKENS, D), jnp.float32)
    return drawn_draw.astype(jnp.bfloat16)


def drawn_weight(key, salt, column_count):
    weight_key = jax.random.fold_in(key, salt)
    entries = jax.random.truncated_normal(weight_key, -6.0, 6.0, (D, column_count), jnp.float32) * D ** (-0.5)
    return entries.astype(jnp.bfloat16)


def draw_w_query(key, part):
    return drawn_weight(key, 23, HEADS * HEAD_DIM)


def draw_w_key(key, part):
    return drawn_weight(key, 37, KV_HEADS * HEAD_DIM)


def shard_levels(stream_key, extent, cuts, low, high):
    gain, own = 1.0, jax.random.fold_in(stream_key, 6)
    for dim, shards_of in cuts:
        steps = jnp.exp(jax.random.uniform(jax.random.fold_in(own, dim), (shards_of,), jnp.float32, low / len(cuts), high / len(cuts)))
        gain = gain * jnp.repeat(steps, extent[dim] // shards_of).reshape([-1 if axis == dim else 1 for axis in range(len(extent))])
    return gain


def noise(own_key, extent, width, reach, shards=(), held_as=jnp.bfloat16):
    values = jax.random.normal(own_key, extent, jnp.float32) * width
    if len(shards) > 0:
        values = shard_levels(own_key, extent, shards, -0.22, 0.18) * values
    return jnp.clip(values, min=-reach, max=reach).astype(held_as)


def setup_inputs(seed: int = 0) -> dict:
    key_list = jax.random.split(jax.random.key(seed), 12)
    return {
        "inputs": draw_inputs(jax.random.fold_in(key_list[11], 71), 0),
        "cotangent": noise(key_list[1], (TOKENS, D), 1.0, 6.0, ((0, 32),)),
        "w_query": draw_w_query(jax.random.fold_in(key_list[11], 71), 0),
        "w_key": draw_w_key(jax.random.fold_in(key_list[11], 71), 0),
        "w_value": noise(key_list[4], (D, KV_HEADS * HEAD_DIM), D ** -0.5, 0.1875, ((0, 4), (1, 8))),
        "w_output": noise(key_list[5], (HEADS * HEAD_DIM, D), (HEADS * HEAD_DIM // 16) ** -0.5, 0.75, ((0, 4), (1, 8))),
        "w_gate": noise(key_list[6], (D, FF), D ** -0.5, 0.1875, ((0, 4), (1, 8))),
        "w_up": noise(key_list[7], (D, FF), D ** -0.5, 0.1875, ((0, 4), (1, 8))),
        "w_down": noise(key_list[8], (FF, D), FF ** -0.5, 0.125, ((0, 4), (1, 8))),
        "gain_attn": jnp.clip(1.0 + 0.1 * jax.random.normal(key_list[9], (D,), jnp.float32), 0.5, 1.5).astype(jnp.bfloat16),
        "gain_ffn": jnp.clip(1.0 + 0.1 * jax.random.normal(key_list[10], (D,), jnp.float32), 0.5, 1.5).astype(jnp.bfloat16),
    }


epsilon = 1e-05
rope_base = 10000.0

def rope_tables(first_pos, row_count, head_width):
    half_width = head_width // 2
    frequency = rope_base ** (-jnp.arange(half_width).astype(jnp.float32) * 2.0 / head_width)
    positions = (first_pos + jnp.arange(row_count)).astype(jnp.float32)
    angles = positions[:, None] * frequency[None, :]
    return (jnp.cos(angles), jnp.sin(angles))

def rotate(vectors, cosine_t, sine_t):
    half_width = vectors.shape[-1] // 2
    lower_half = vectors[..., :half_width]
    upper_half = vectors[..., half_width:]
    cos_b = cosine_t[:, None, :]
    sin_b = sine_t[:, None, :]
    return jnp.concatenate([lower_half * cos_b - upper_half * sin_b, upper_half * cos_b + lower_half * sin_b], axis=-1)

def unrotate(vectors, cosine_t, sine_t):
    half_width = vectors.shape[-1] // 2
    lower_half = vectors[..., :half_width]
    upper_half = vectors[..., half_width:]
    cos_b = cosine_t[:, None, :]
    sin_b = sine_t[:, None, :]
    return jnp.concatenate([lower_half * cos_b + upper_half * sin_b, upper_half * cos_b - lower_half * sin_b], axis=-1)

def norm_forward(hidden, gain_vec):
    inverse = lax.rsqrt(lax.optimization_barrier(jnp.mean(hidden * hidden, axis=-1, keepdims=True)) + epsilon)
    return (hidden * inverse * gain_vec, inverse)

def norm_backward(hidden, inverse, gain_vec, upstream):
    scaled = upstream * gain_vec
    feature_count = hidden.shape[-1]
    cubed = inverse * inverse * inverse
    d_hidden = inverse * scaled - hidden * cubed * lax.optimization_barrier(jnp.sum(scaled * hidden, axis=-1, keepdims=True)) / feature_count
    d_gain = lax.optimization_barrier(jnp.sum(upstream * hidden * inverse, axis=0))
    return (d_hidden, d_gain)

def rounded(vectors):
    return lax.optimization_barrier(vectors.astype(jnp.bfloat16)).astype(jnp.float32)

def one_sequence(weights, gain_pair, inputs, cotangent):
    w_query, w_key, w_value, w_output, w_gate, w_up, w_down = weights
    gain_one = gain_pair[0].astype(jnp.float32)
    gain_two = gain_pair[1].astype(jnp.float32)
    length = inputs.shape[0]
    group_size = HEADS // KV_HEADS
    score_scale = HEAD_DIM ** (-0.5)
    block_count = length // TOK_DEV
    cosine_t, sine_t = rope_tables(0, length, HEAD_DIM)
    hidden = inputs.astype(jnp.float32)
    normed_f, inv_one = norm_forward(hidden, gain_one)
    normed_one = normed_f.astype(jnp.bfloat16)
    query_pre = jnp.dot(normed_one, w_query, preferred_element_type=jnp.float32).reshape(length, HEADS, HEAD_DIM)
    queries = rotate(query_pre, cosine_t, sine_t).astype(jnp.bfloat16).reshape(length, KV_HEADS, group_size, HEAD_DIM)
    key_pre = jnp.dot(normed_one, w_key, preferred_element_type=jnp.float32).reshape(length, KV_HEADS, HEAD_DIM)
    key_heads = rotate(key_pre, cosine_t, sine_t).astype(jnp.bfloat16)
    value_heads = jnp.dot(normed_one, w_value, preferred_element_type=jnp.float32).astype(jnp.bfloat16).reshape(length, KV_HEADS, HEAD_DIM)
    key_f = key_heads.astype(jnp.float32)
    value_f = value_heads.astype(jnp.float32)
    key_pos = jnp.arange(length).astype(jnp.int32)

    def scores_for(block_index):
        first_row = (block_index * TOK_DEV).astype(jnp.int32)
        query_block = lax.dynamic_slice_in_dim(queries, first_row, TOK_DEV, 0).astype(jnp.float32)
        raw_scores = jnp.einsum('tkgd,skd->kgts', query_block, key_f) * score_scale
        query_pos = first_row + jnp.arange(TOK_DEV).astype(jnp.int32)
        allowed = query_pos[:, None] >= key_pos[None, :]
        return (jnp.where(allowed, raw_scores, -1e+30), query_block)

    def forward_block(block_index):
        masked, query_block = scores_for(block_index)
        row_max = lax.optimization_barrier(jnp.max(masked, axis=-1))
        expo = jnp.exp(masked - row_max[..., None])
        weight_sum = lax.optimization_barrier(jnp.sum(expo, axis=-1))
        mixed_heads = jnp.einsum('kgts,skd->kgtd', rounded(expo), value_f) / weight_sum[..., None]
        return (mixed_heads.astype(jnp.bfloat16), row_max + jnp.log(weight_sum))
    block_ids = jnp.arange(block_count).astype(jnp.int32)
    attended_blocks, logsum = lax.map(forward_block, block_ids)
    attended = jnp.transpose(attended_blocks, (0, 3, 1, 2, 4)).reshape(length, HEADS * HEAD_DIM)
    middle = hidden + jnp.dot(attended, w_output, preferred_element_type=jnp.float32)
    normed_g, inv_two = norm_forward(middle, gain_two)
    normed_two = normed_g.astype(jnp.bfloat16)
    gate_pre = jnp.dot(normed_two, w_gate, preferred_element_type=jnp.float32)
    up_pre = jnp.dot(normed_two, w_up, preferred_element_type=jnp.float32)
    sigma = jax.nn.sigmoid(gate_pre)
    silu_gate = gate_pre * sigma
    mixed_act = (silu_gate * up_pre).astype(jnp.bfloat16)
    result = middle + jnp.dot(mixed_act, w_down, preferred_element_type=jnp.float32)
    out_act = result.astype(jnp.bfloat16)
    cot_f = cotangent.astype(jnp.float32)
    grad_down = jnp.dot(mixed_act.T, cotangent, preferred_element_type=jnp.float32)
    d_mixed = jnp.dot(cotangent, w_down.T, preferred_element_type=jnp.float32)
    d_gate = (d_mixed * up_pre * sigma * (1.0 + gate_pre * (1.0 - sigma))).astype(jnp.bfloat16)
    d_up = (d_mixed * silu_gate).astype(jnp.bfloat16)
    grad_gate = jnp.dot(normed_two.T, d_gate, preferred_element_type=jnp.float32)
    grad_up = jnp.dot(normed_two.T, d_up, preferred_element_type=jnp.float32)
    d_norm_two = jnp.dot(d_gate, w_gate.T, preferred_element_type=jnp.float32) + jnp.dot(d_up, w_up.T, preferred_element_type=jnp.float32)
    d_mid_norm, grad_gain_two = norm_backward(middle, inv_two, gain_two, d_norm_two)
    d_middle = cot_f + d_mid_norm
    d_middle_b = d_middle.astype(jnp.bfloat16)
    grad_output = jnp.dot(attended.T, d_middle_b, preferred_element_type=jnp.float32)
    d_attended = jnp.dot(d_middle_b, w_output.T, preferred_element_type=jnp.float32).astype(jnp.bfloat16)
    grad_heads = d_attended.reshape(length, KV_HEADS, group_size, HEAD_DIM)
    attended_heads = attended.reshape(length, KV_HEADS, group_size, HEAD_DIM)

    def backward_block(loop_carry, block_index):
        grad_keys, grad_values = loop_carry
        masked, query_block = scores_for(block_index)
        first_row = (block_index * TOK_DEV).astype(jnp.int32)
        grad_block = lax.dynamic_slice_in_dim(grad_heads, first_row, TOK_DEV, 0).astype(jnp.float32)
        att_block = lax.dynamic_slice_in_dim(attended_heads, first_row, TOK_DEV, 0).astype(jnp.float32)
        delta_rows = jnp.einsum('tkgd,tkgd->kgt', grad_block, att_block)
        probs = jnp.exp(masked - logsum[block_index][..., None])
        grad_values = grad_values + jnp.einsum('kgts,tkgd->skd', rounded(probs), grad_block)
        grad_probs = jnp.einsum('tkgd,skd->kgts', grad_block, value_f)
        d_scores = rounded(probs * (grad_probs - delta_rows[..., None]))
        grad_query = jnp.einsum('kgts,skd->tkgd', d_scores, key_f) * score_scale
        grad_keys = grad_keys + jnp.einsum('kgts,tkgd->skd', d_scores, query_block) * score_scale
        return ((grad_keys, grad_values), grad_query)
    zero_kv = jnp.zeros((length, KV_HEADS, HEAD_DIM), jnp.float32)
    (grad_keys, grad_values), grad_query = lax.scan(backward_block, (zero_kv, zero_kv), block_ids)
    grad_query = grad_query.reshape(length, HEADS, HEAD_DIM)
    dq_in = unrotate(grad_query, cosine_t, sine_t).astype(jnp.bfloat16).reshape(length, HEADS * HEAD_DIM)
    dk_in = unrotate(grad_keys, cosine_t, sine_t).astype(jnp.bfloat16).reshape(length, KV_HEADS * HEAD_DIM)
    dv_in = grad_values.astype(jnp.bfloat16).reshape(length, KV_HEADS * HEAD_DIM)
    grad_wq = jnp.dot(normed_one.T, dq_in, preferred_element_type=jnp.float32)
    grad_wk = jnp.dot(normed_one.T, dk_in, preferred_element_type=jnp.float32)
    grad_wv = jnp.dot(normed_one.T, dv_in, preferred_element_type=jnp.float32)
    d_norm_one = jnp.dot(dq_in, w_query.T, preferred_element_type=jnp.float32)
    d_norm_one = d_norm_one + jnp.dot(dk_in, w_key.T, preferred_element_type=jnp.float32)
    d_norm_one = d_norm_one + jnp.dot(dv_in, w_value.T, preferred_element_type=jnp.float32)
    d_in_norm, grad_gain_one = norm_backward(hidden, inv_one, gain_one, d_norm_one)
    grad_input = d_middle + d_in_norm
    grads = (grad_wq, grad_wk, grad_wv, grad_output, grad_gate, grad_up, grad_down, grad_gain_one, grad_gain_two)
    return (out_act, grad_input, grads)

def reference(inputs, cotangent, w_query, w_key, w_value, w_output, w_gate, w_up, w_down, gain_attn, gain_ffn):
    weights = (w_query, w_key, w_value, w_output, w_gate, w_up, w_down)
    gain_pair = (gain_attn, gain_ffn)
    seq_inputs = inputs.reshape(SEQS, LENGTH, D)
    seq_cot = cotangent.reshape(SEQS, LENGTH, D)
    zero_grads = tuple((jnp.zeros(weight.shape, jnp.float32) for weight in weights + gain_pair))

    def seq_step(loop_carry, seq_pair):
        out_act, grad_input, grads = one_sequence(weights, gain_pair, seq_pair[0], seq_pair[1])
        summed = tuple((left + right for left, right in zip(loop_carry, grads)))
        return (summed, (out_act, grad_input))
    totals, (outs, grad_ins) = lax.scan(seq_step, zero_grads, (seq_inputs, seq_cot))
    return (outs.reshape(TOKENS, D), grad_ins.reshape(TOKENS, D), totals[0], totals[1], totals[2], totals[3], totals[4], totals[5], totals[6], totals[7], totals[8])
```

```python
import functools

import jax
import jax.numpy as jnp
from jax import lax
from jax.experimental import pallas as pl
from jax.experimental.pallas import tpu as pltpu
from jax.sharding import PartitionSpec as P

HEADS = 15
KV_HEADS = 5
HEAD_DIM = 64
GROUP = HEADS // KV_HEADS

epsilon = 1e-05
rope_base = 10000.0
bf16 = jnp.bfloat16
f32 = jnp.float32


def remote(src, dst, send, recv, axis, peer):
    return pltpu.make_async_remote_copy(
        src_ref=src,
        dst_ref=dst,
        send_sem=send,
        recv_sem=recv,
        device_id={axis: peer},
        device_id_type=pl.DeviceIdType.MESH,
    )


class Gather:
    def __init__(self, axis, array):
        self.axis, self.array = axis, array

    def plan(self, sizes):
        self.n = sizes[self.axis]
        self.pairs = self.axis == "ctx"
        self.out = jax.ShapeDtypeStruct((self.n,) + self.array.shape, self.array.dtype)
        self.scratch = [pltpu.SemaphoreType.DMA((self.n,))] * 4 + [pltpu.SemaphoreType.DMA(())]

    def start(self, src, dst, send, recv, fsend, frecv, own):
        me = lax.axis_index(self.axis)
        self.copies = []
        local = pltpu.make_async_copy(src, dst.at[me], own)
        local.start()
        self.local = local
        if self.pairs:
            chips = self.n // 2
            chip, core = me // 2, me % 2
            self.hops = []
            for k in range(1, chips):
                peer = lax.rem(chip + k, chips) * 2 + core
                copy = remote(src, dst.at[me], send.at[k], recv.at[k], self.axis, peer)
                copy.start()
                self.copies.append(copy)
            partner = me + 1 - 2 * core
            copy = remote(src, dst.at[me], fsend.at[0], frecv.at[0], self.axis, partner)
            copy.start()
            self.copies.append(copy)
        else:
            for k in range(1, self.n):
                peer = lax.rem(me + k, self.n)
                copy = remote(src, dst.at[me], send.at[k], recv.at[k], self.axis, peer)
                copy.start()
                self.copies.append(copy)

    def middle(self, src, dst, send, recv, fsend, frecv, own):
        if not self.pairs:
            return
        me = lax.axis_index(self.axis)
        chips = self.n // 2
        chip, core = me // 2, me % 2
        partner = me + 1 - 2 * core
        for k in range(1, chips):
            slot = lax.rem(chip + chips - k, chips) * 2 + core
            remote(src, dst.at[slot], send.at[k], recv.at[k], self.axis, partner).wait_recv()
            copy = remote(dst.at[slot], dst.at[slot], fsend.at[k], frecv.at[k], self.axis, partner)
            copy.start()
            self.copies.append(copy)

    def finish(self, src, dst, send, recv, fsend, frecv, own):
        me = lax.axis_index(self.axis)
        if self.pairs:
            chips = self.n // 2
            chip, core = me // 2, me % 2
            partner = me + 1 - 2 * core
            for k in range(chips):
                slot = lax.rem(chip + chips - k, chips) * 2 + 1 - core
                remote(
                    src, dst.at[slot], fsend.at[k], frecv.at[k], self.axis, partner
                ).wait_recv()
        else:
            for k in range(1, self.n):
                slot = lax.rem(me + self.n - k, self.n)
                remote(src, dst.at[slot], send.at[k], recv.at[k], self.axis, slot).wait_recv()
        for copy in self.copies:
            copy.wait_send()
        self.local.wait()


class Swap:
    def __init__(self, axis, array):
        self.axis, self.array = axis, array

    def plan(self, sizes):
        self.n = sizes[self.axis]
        self.out = jax.ShapeDtypeStruct(self.array.shape, self.array.dtype)
        self.scratch = [pltpu.SemaphoreType.DMA((self.n,))] * 2 + [pltpu.SemaphoreType.DMA(())]

    def start(self, src, dst, send, recv, own):
        me = lax.axis_index(self.axis)
        self.local = pltpu.make_async_copy(src.at[me], dst.at[me], own)
        self.local.start()
        self.copies = []
        for k in range(1, self.n):
            peer = lax.rem(me + k, self.n)
            copy = remote(src.at[peer], dst.at[me], send.at[k], recv.at[k], self.axis, peer)
            copy.start()
            self.copies.append(copy)

    def middle(self, *refs):
        pass

    def finish(self, src, dst, send, recv, own):
        me = lax.axis_index(self.axis)
        for k in range(1, self.n):
            slot = lax.rem(me + self.n - k, self.n)
            remote(
                src.at[slot], dst.at[slot], send.at[k], recv.at[k], self.axis, slot
            ).wait_recv()
        for copy in self.copies:
            copy.wait_send()
        self.local.wait()


class Shift:
    def __init__(self, axis, array, by):
        self.axis, self.array, self.by = axis, array, by

    def plan(self, sizes):
        self.n = sizes[self.axis]
        self.out = jax.ShapeDtypeStruct(self.array.shape, self.array.dtype)
        self.scratch = [pltpu.SemaphoreType.DMA(())] * 2

    def start(self, src, dst, send, recv):
        me = lax.axis_index(self.axis)
        peer = lax.rem(me + self.n + self.by, self.n)
        self.copy = remote(src, dst, send, recv, self.axis, peer)
        self.copy.start()

    def middle(self, *refs):
        pass

    def finish(self, *refs):
        self.copy.wait_recv()
        self.copy.wait_send()


class Reduce:
    axis = "ctx"

    def __init__(self, array):
        self.array = array

    def plan(self, sizes):
        self.n = sizes[self.axis]
        block = self.array.shape[1:]
        chips = self.n // 2
        self.out = jax.ShapeDtypeStruct(block, f32)
        slots = pltpu.VMEM((chips,) + block, self.array.dtype)
        self.scratch = [pltpu.SemaphoreType.DMA((chips,))] * 4 + [slots] * 3

    def start(self, src, dst, psend, precv, send, recv, near, term, far):
        me = lax.axis_index(self.axis)
        chips = self.n // 2
        chip, core = me // 2, me % 2
        partner = me + 1 - 2 * core
        self.copies = []
        for k in list(range(1, chips)) + [0]:
            slot = lax.rem(chip + k, chips) * 2 + 1 - core
            copy = remote(
                src.at[slot], near.at[k], psend.at[k], precv.at[k], self.axis, partner
            )
            copy.start()
            self.copies.append(copy)

    def middle(self, src, dst, psend, precv, send, recv, near, term, far):
        me = lax.axis_index(self.axis)
        chips = self.n // 2
        chip, core = me // 2, me % 2
        partner = me + 1 - 2 * core
        for k in range(1, chips):
            remote(
                src.at[me], near.at[k], psend.at[k], precv.at[k], self.axis, partner
            ).wait_recv()
            peer = lax.rem(chip + k, chips) * 2 + core
            both = src[peer].astype(f32) + near[k].astype(f32)
            term[k] = both.astype(term.dtype)
            copy = remote(term.at[k], far.at[k], send.at[k], recv.at[k], self.axis, peer)
            copy.start()
            self.copies.append(copy)

    def finish(self, src, dst, psend, precv, send, recv, near, term, far):
        me = lax.axis_index(self.axis)
        chips = self.n // 2
        core = me % 2
        partner = me + 1 - 2 * core
        remote(src.at[me], near.at[0], psend.at[0], precv.at[0], self.axis, partner).wait_recv()
        dst[...] = src[me].astype(f32) + near[0].astype(f32)
        for k in range(1, chips):
            remote(
                src.at[me], far.at[k], send.at[k], recv.at[k], self.axis, partner
            ).wait_recv()
            dst[...] += far[k].astype(f32)
        for copy in self.copies:
            copy.wait_send()


def exchange(ident, *tasks):
    sizes = {axis: lax.axis_size(axis) for axis in ("dp", "ctx")}
    for task in tasks:
        task.plan(sizes)
    axes = [axis for axis in ("dp", "ctx") if any(task.axis == axis for task in tasks)]
    count = len(tasks)

    def kernel(*refs):
        barrier = pltpu.get_barrier_semaphore()
        greeted = 0
        for axis in axes:
            me, n = lax.axis_index(axis), sizes[axis]
            for k in range(1, n):
                pl.semaphore_signal(
                    barrier,
                    inc=1,
                    device_id={axis: lax.rem(me + k, n)},
                    device_id_type=pl.DeviceIdType.MESH,
                )
            greeted += n - 1
        pl.semaphore_wait(barrier, greeted)
        held, at = [], 2 * count
        for i, task in enumerate(tasks):
            held.append((refs[i], refs[count + i]) + tuple(refs[at : at + len(task.scratch)]))
            at += len(task.scratch)
        for task, own in zip(tasks, held):
            task.start(*own)
        for task, own in zip(tasks, held):
            task.middle(*own)
        for task, own in zip(tasks, held):
            task.finish(*own)

    return pl.pallas_call(
        kernel,
        out_shape=[task.out for task in tasks],
        in_specs=[pl.BlockSpec(memory_space=pltpu.VMEM)] * count,
        out_specs=[pl.BlockSpec(memory_space=pltpu.VMEM)] * count,
        scratch_shapes=[shape for task in tasks for shape in task.scratch],
        compiler_params=pltpu.CompilerParams(
            collective_id=ident, has_side_effects=True, vmem_limit_bytes=60 * 1024 * 1024
        ),
        name=f"exchange_{ident}",
    )(*[task.array for task in tasks])


def mm(a, b, dims):
    return lax.dot_general(a, b, ((dims[:1], dims[1:]), ((), ())), preferred_element_type=f32)


def nn(a, b):
    return mm(a, b, (1, 0))


def nt(a, b):
    return mm(a, b, (1, 1))


def tn(a, b):
    return mm(a, b, (0, 0))


def turned(rows):
    width = rows.shape[-1]
    parts = rows.reshape(-1, 2, HEAD_DIM // 2, width)
    return jnp.concatenate([-parts[:, 1:], parts[:, :1]], axis=1).reshape(rows.shape)


def rope_tables(row_count):
    half = HEAD_DIM // 2
    frequency = rope_base ** (-jnp.arange(half).astype(f32) * 2.0 / HEAD_DIM)
    angles = jnp.arange(row_count).astype(f32)[:, None] * frequency[None, :]
    return jnp.tile(jnp.cos(angles), (1, 2)), jnp.tile(jnp.sin(angles), (1, 2))


def norm_backward(hidden, inverse, gain_vec, upstream):
    scaled = upstream * gain_vec
    cubed = inverse * inverse * inverse
    d_hidden = (
        inverse * scaled
        - hidden
        * cubed
        * jnp.sum(scaled * hidden, axis=-1, keepdims=True)
        / hidden.shape[-1]
    )
    return d_hidden, jnp.sum(upstream * hidden * inverse, axis=0)


def inverse_rms(hidden):
    return lax.rsqrt(jnp.mean(hidden * hidden, axis=-1, keepdims=True) + epsilon)


def masked_scores(queries, keys, first):
    scores = nt(queries, keys) * HEAD_DIM ** (-0.5)
    rows = first + lax.broadcasted_iota(jnp.int32, scores.shape, 0)
    return jnp.where(rows >= lax.broadcasted_iota(jnp.int32, scores.shape, 1), scores, -1e30)


def shards(
    inputs, cotangent, w_query, w_key, w_value, w_output, w_gate, w_up, w_down, gain_attn, gain_ffn
):
    dp, ctx = lax.axis_size("dp"), lax.axis_size("ctx")
    me = lax.axis_index("ctx")
    rows, width = inputs.shape
    length = rows * ctx
    q_w, k_w, o_w, f_w = w_query.shape[1], w_key.shape[1], w_output.shape[1], w_gate.shape[1]
    in_rows = w_query.shape[0]
    held = -(-HEADS // ctx)
    wide = held * HEAD_DIM
    total = ctx * wide
    near = all(wide * j >= q_w * j and wide * (j + 1) <= q_w * (j + 2) for j in range(ctx))

    packed = jnp.concatenate([w_gate, w_up, w_query, w_key, w_value, w_output], axis=1)
    gains = jnp.stack([gain_attn, gain_ffn])
    packed, all_down, all_x, all_gains = exchange(
        0,
        Gather("dp", packed),
        Gather("dp", w_down),
        Gather("ctx", inputs),
        Gather("ctx", gains),
    )
    packed = packed.reshape(dp * in_rows, packed.shape[2])
    w_gu = packed[:, : 2 * f_w]
    turned_w = packed[:, 2 * f_w :].T
    q_part = turned_w[:q_w]
    kv_part = turned_w[q_w : q_w + 2 * k_w]
    o_part = jnp.pad(turned_w[q_w + 2 * k_w :], ((0, 0), (0, total - HEADS * HEAD_DIM)))
    o_part = o_part.reshape(o_w, ctx, wide).transpose(1, 0, 2)
    down_part = all_down.reshape(ctx, -1, o_w)

    kv_all, q_next, o_mine, down_mine, all_cot = exchange(
        1,
        Gather("ctx", kv_part),
        Shift("ctx", q_part, -1) if near else Gather("ctx", q_part),
        Swap("ctx", o_part),
        Swap("ctx", down_part),
        Gather("ctx", cotangent),
    )
    if near:
        q_rows = jnp.concatenate(
            [q_part, jnp.where(me == ctx - 1, jnp.zeros_like(q_next), q_next)], axis=0
        )
        q_rows = jnp.pad(q_rows, ((0, wide), (0, 0)))
        wq = lax.dynamic_slice(q_rows, (me * (wide - q_w), 0), (wide, width))
    else:
        q_rows = jnp.pad(q_next.reshape(-1, width), ((0, total - HEADS * HEAD_DIM), (0, 0)))
        wq = lax.dynamic_slice(q_rows, (me * wide, 0), (wide, width))
    wk_all = kv_all[:, :k_w].reshape(-1, width)
    wv_all = kv_all[:, k_w:].reshape(-1, width)
    kv_head = [jnp.minimum((me * held + h) // GROUP, KV_HEADS - 1) for h in range(held)]

    def of_heads(array):
        return jnp.concatenate(
            [lax.dynamic_slice(array, (k * HEAD_DIM, 0), (HEAD_DIM, width)) for k in kv_head]
        )

    wk, wv = of_heads(wk_all), of_heads(wv_all)
    wo = o_mine.reshape(ctx * o_w, wide)
    w_down_t = down_mine.transpose(0, 2, 1).reshape(ctx * o_w, f_w)
    gain_rows = all_gains.transpose(1, 0, 2).reshape(2, width).astype(f32)
    gain_one, gain_two = gain_rows[0], gain_rows[1]

    x_full = all_x.reshape(length, width)
    cot_full = all_cot.reshape(length, width)
    hid_full = x_full.astype(f32)
    normed_one = (hid_full * inverse_rms(hid_full) * gain_one).astype(bf16)
    cosine, sine = rope_tables(length)
    cosine, sine = jnp.tile(cosine, (1, held)), jnp.tile(sine, (1, held))
    projected = nt(normed_one, jnp.concatenate([wq, turned(wq), wk, turned(wk), wv]))
    q_a, q_b, k_a, k_b, v_a = [projected[:, i * wide : (i + 1) * wide] for i in range(5)]
    queries = (q_a * cosine + q_b * sine).astype(bf16)
    q_side = (q_a * sine - q_b * cosine).astype(bf16)
    keys = (k_a * cosine + k_b * sine).astype(bf16)
    k_side = (k_a * sine - k_b * cosine).astype(bf16)
    values = v_a.astype(bf16)

    def head(array, h):
        return array[:, h * HEAD_DIM : (h + 1) * HEAD_DIM]

    chunk = min(256, length)
    firsts = list(range(0, length, chunk))
    attended, logsums = [], []
    for h in range(held):
        q_h, k_h, v_h = head(queries, h), head(keys, h), head(values, h)
        outs, logs = [], []
        for first in firsts:
            last = first + chunk
            scores = masked_scores(q_h[first:last], k_h[:last], first)
            top = jnp.max(scores, axis=-1, keepdims=True)
            expo = jnp.exp(scores - top)
            weight = jnp.sum(expo, axis=-1, keepdims=True)
            outs.append(nn(expo.astype(bf16), v_h[:last]) / weight)
            logs.append(top + jnp.log(weight))
        real = me * held + h < HEADS
        attended.append(jnp.where(real, jnp.concatenate(outs), 0.0).astype(bf16))
        logsums.append(logs)
    attended_all = jnp.concatenate(attended, axis=1)

    (mid_sum,) = exchange(2, Reduce(nt(attended_all, wo).astype(bf16).reshape(ctx, rows, width)))
    hidden = inputs.astype(f32)
    middle = hidden + mid_sum
    inv_two = inverse_rms(middle)
    normed_two_mine = (middle * inv_two * gain_two).astype(bf16)
    (normed_two,) = exchange(3, Gather("ctx", normed_two_mine))
    normed_two = normed_two.reshape(length, width)

    both = nn(normed_two, w_gu)
    gate_pre, up_pre = both[:, :f_w], both[:, f_w:]
    d_mixed = nn(cot_full, w_down_t)
    sigma = jax.nn.sigmoid(gate_pre)
    silu_gate = gate_pre * sigma
    mixed_act = (silu_gate * up_pre).astype(bf16)
    d_gate = (d_mixed * up_pre * sigma * (1.0 + gate_pre * (1.0 - sigma))).astype(bf16)
    d_up = (d_mixed * silu_gate).astype(bf16)
    d_both = jnp.concatenate([d_gate, d_up], axis=1)
    out_part = nt(mixed_act, w_down_t).astype(bf16)
    d_two_part = nt(d_both, w_gu).astype(bf16)
    g_down = tn(cot_full, mixed_act).astype(bf16)
    g_gu = tn(normed_two, d_both).astype(bf16)

    d_norm_two, g_gu_all = exchange(
        4,
        Reduce(d_two_part.reshape(ctx, rows, width)),
        Swap("dp", g_gu.reshape(dp, in_rows, 2 * f_w)),
    )
    g_gu_sum = jnp.sum(g_gu_all.astype(f32), axis=0)
    d_mid_norm, g_gain_two = norm_backward(middle, inv_two, gain_two, d_norm_two)
    d_middle = cotangent.astype(f32) + d_mid_norm
    d_mid_full, g_down_all, out_sum = exchange(
        5,
        Gather("ctx", d_middle.astype(bf16)),
        Swap("ctx", g_down.reshape(ctx, o_w, f_w)),
        Reduce(out_part.reshape(ctx, rows, width)),
    )
    out_act = (middle + out_sum).astype(bf16)
    d_mid_full = d_mid_full.reshape(length, width)
    g_down_all = g_down_all.transpose(0, 2, 1).reshape(dp, -1, o_w)

    g_out = tn(d_mid_full, attended_all).astype(bf16)
    d_attended = nn(d_mid_full, wo).astype(bf16)
    dq_all, dk_all, dv_all = [], [], []
    for h in range(held):
        q_h, k_h, v_h = head(queries, h), head(keys, h), head(values, h)
        q_two = jnp.concatenate([q_h, head(q_side, h)], axis=1)
        k_two = jnp.concatenate([k_h, head(k_side, h)], axis=1)
        grad_h = head(d_attended, h)
        delta = jnp.sum(grad_h.astype(f32) * attended[h].astype(f32), axis=-1, keepdims=True)
        dq_parts = []
        dk = jnp.zeros((length, 2 * HEAD_DIM), f32)
        dv = jnp.zeros((length, HEAD_DIM), f32)
        for i, first in enumerate(firsts):
            last = first + chunk
            probs = jnp.exp(masked_scores(q_h[first:last], k_h[:last], first) - logsums[h][i])
            d_probs = nt(grad_h[first:last], v_h[:last])
            d_scores = (probs * (d_probs - delta[first:last])).astype(bf16)
            dq_parts.append(nn(d_scores, k_two[:last]))
            tail = ((0, length - last), (0, 0))
            dk = dk + jnp.pad(tn(d_scores, q_two[first:last]), tail)
            dv = dv + jnp.pad(tn(probs.astype(bf16), grad_h[first:last]), tail)
        dq = jnp.concatenate(dq_parts)
        real = me * held + h < HEADS
        cos_h, sin_h = head(cosine, 0), head(sine, 0)

        def back(two):
            turned_back = two[:, :HEAD_DIM] * cos_h + two[:, HEAD_DIM:] * sin_h
            return jnp.where(real, turned_back * HEAD_DIM ** (-0.5), 0.0).astype(bf16)

        dq_all.append(back(dq))
        dk_all.append(back(dk))
        dv_all.append(jnp.where(real, dv, 0.0).astype(bf16))
    d_qkv = jnp.concatenate(dq_all + dk_all + dv_all, axis=1)
    d_one_part = nn(d_qkv, jnp.concatenate([wq, wk, wv])).astype(bf16)
    g_qkv = tn(d_qkv, normed_one).astype(bf16)
    g_qkv = g_qkv.reshape(3 * wide, dp, in_rows).transpose(1, 0, 2)

    d_norm_one, g_out_all, g_qkv_all, g_down_mine = exchange(
        6,
        Reduce(d_one_part.reshape(ctx, rows, width)),
        Swap("ctx", g_out.reshape(ctx, o_w, wide)),
        Swap("dp", g_qkv),
        Swap("dp", g_down_all),
    )
    inv_one = inverse_rms(hidden)
    d_in_norm, g_gain_one = norm_backward(hidden, inv_one, gain_one, d_norm_one)
    grad_input = d_middle + d_in_norm
    g_down_sum = jnp.sum(g_down_mine.astype(f32), axis=0)
    g_qkv_sum = jnp.sum(g_qkv_all.astype(f32), axis=0)
    gq_part = g_qkv_sum[:wide].astype(bf16)
    g_kv = jnp.zeros((2, KV_HEADS * HEAD_DIM, in_rows), f32)
    for kind in range(2):
        for h in range(held):
            at = (kind, kv_head[h] * HEAD_DIM, 0)
            base = (1 + kind) * wide + h * HEAD_DIM
            block = lax.dynamic_slice(g_kv, at, (1, HEAD_DIM, in_rows))
            g_kv = lax.dynamic_update_slice(
                g_kv, block + g_qkv_sum[None, base : base + HEAD_DIM], at
            )
    g_kv = g_kv.astype(bf16).reshape(2, ctx, k_w, in_rows).transpose(1, 0, 2, 3)
    g_kv = g_kv.reshape(ctx, 2 * k_w, in_rows)
    g_out_rows = g_out_all.transpose(0, 2, 1).reshape(total, o_w)[: HEADS * HEAD_DIM]
    g_gain = jnp.stack([g_gain_one, g_gain_two]).reshape(2, ctx, -1).transpose(1, 0, 2)
    if near:
        q_task = Shift("ctx", gq_part, 1)
    else:
        q_place = lax.dynamic_update_slice(
            jnp.zeros((total, in_rows), bf16), gq_part, (me * wide, 0)
        )
        q_task = Reduce(q_place[: HEADS * HEAD_DIM].reshape(ctx, q_w, in_rows))
    kv_sum, q_got, g_out_mine, gain_all = exchange(
        7,
        Reduce(g_kv),
        q_task,
        Swap("dp", g_out_rows.reshape(dp, in_rows, o_w)),
        Swap("ctx", g_gain),
    )
    if near:
        q_rows = jnp.concatenate([q_got, gq_part], axis=0)
        g_query = lax.dynamic_slice(
            q_rows, (wide - me * (wide - q_w), 0), (q_w, in_rows)
        ).astype(f32)
    else:
        g_query = q_got
    gain_sum = lax.psum(jnp.sum(gain_all, axis=0), "dp")
    return (
        out_act,
        grad_input,
        g_query.T,
        kv_sum[:k_w].T,
        kv_sum[k_w:].T,
        jnp.sum(g_out_mine.astype(f32), axis=0),
        g_gu_sum[:, :f_w],
        g_gu_sum[:, f_w:],
        g_down_sum,
        gain_sum[0],
        gain_sum[1],
    )


def solution(mesh):
    blocks = P(("dp", "ctx"), None)
    matrix = P("dp", "ctx")
    in_specs = (blocks,) * 2 + (matrix,) * 7 + (P("ctx"),) * 2
    return jax.shard_map(shards, mesh=mesh, in_specs=in_specs, out_specs=in_specs, check_vma=False)
```

```python
import functools

import jax
import jax.numpy as jnp
from jax import lax
from jax.experimental import pallas as pl
from jax.experimental.pallas import tpu as pltpu
from jax.sharding import PartitionSpec as P

HEADS = 15
KV_HEADS = 5
HEAD_DIM = 64
GROUP = HEADS // KV_HEADS

epsilon = 1e-05
rope_base = 10000.0
bf16 = jnp.bfloat16
f32 = jnp.float32


def remote(src, dst, send, recv, axis, peer):
    return pltpu.make_async_remote_copy(
        src_ref=src,
        dst_ref=dst,
        send_sem=send,
        recv_sem=recv,
        device_id={axis: peer},
        device_id_type=pl.DeviceIdType.MESH,
    )


class Gather:
    axis = "dp"

    def __init__(self, array):
        self.array = array

    def plan(self, sizes):
        self.n = sizes[self.axis]
        self.out = jax.ShapeDtypeStruct((self.n,) + self.array.shape, self.array.dtype)
        self.scratch = [pltpu.SemaphoreType.DMA((self.n,))] * 2 + [pltpu.SemaphoreType.DMA(())]

    def start(self, src, dst, send, recv, own):
        me = lax.axis_index(self.axis)
        self.local = pltpu.make_async_copy(src, dst.at[me], own)
        self.local.start()
        self.copies = []
        for k in range(1, self.n):
            peer = lax.rem(me + k, self.n)
            copy = remote(src, dst.at[me], send.at[k], recv.at[k], self.axis, peer)
            copy.start()
            self.copies.append(copy)

    def middle(self, *refs):
        pass

    def finish(self, src, dst, send, recv, own):
        me = lax.axis_index(self.axis)
        for k in range(1, self.n):
            slot = lax.rem(me + self.n - k, self.n)
            remote(src, dst.at[slot], send.at[k], recv.at[k], self.axis, slot).wait_recv()
        for copy in self.copies:
            copy.wait_send()
        self.local.wait()


class Relay:
    axis = "ctx"

    def __init__(self, array):
        self.array = array

    def plan(self, sizes):
        self.n = sizes[self.axis]
        chips = self.n // 2
        self.out = jax.ShapeDtypeStruct((self.n,) + self.array.shape, self.array.dtype)
        self.scratch = [pltpu.SemaphoreType.DMA((chips,))] * 6 + [pltpu.SemaphoreType.DMA(())]

    def at(self):
        me = lax.axis_index(self.axis)
        chip, core = me // 2, me % 2
        return me, chip, core, me + 1 - 2 * core, self.n // 2

    def start(self, src, dst, rs, rr, ls, lr, ps, pr, own):
        me, chip, core, partner, chips = self.at()

        @pl.when(chip < chips - 1)
        def _():
            remote(src, dst.at[me], rs.at[0], rr.at[0], self.axis, me + 2).start()

        @pl.when(chip > 0)
        def _():
            remote(src, dst.at[me], ls.at[0], lr.at[0], self.axis, me - 2).start()

        remote(src, dst.at[me], ps.at[chip], pr.at[chip], self.axis, partner).start()
        pltpu.make_async_copy(src, dst.at[me], own).start()

    def step(self, k, src, dst, rs, rr, ls, lr, ps, pr, own):
        me, chip, core, partner, chips = self.at()

        def arrived(slot_chip, way, send, recv):
            slot = slot_chip * 2 + core
            back = me - 2 * way
            remote(dst.at[slot], dst.at[slot], send.at[k], recv.at[k], self.axis, back).wait_recv()

            @pl.when(jnp.logical_and(chip + way >= 0, chip + way < chips))
            def _():
                remote(
                    dst.at[slot],
                    dst.at[slot],
                    send.at[k + 1],
                    recv.at[k + 1],
                    self.axis,
                    me + 2 * way,
                ).start()

            remote(
                dst.at[slot], dst.at[slot], ps.at[slot_chip], pr.at[slot_chip], self.axis, partner
            ).start()

        @pl.when(chip - 1 - k >= 0)
        def _():
            arrived(chip - 1 - k, 1, rs, rr)

        @pl.when(chip + 1 + k < chips)
        def _():
            arrived(chip + 1 + k, -1, ls, lr)

    def finish(self, src, dst, rs, rr, ls, lr, ps, pr, own):
        me, chip, core, partner, chips = self.at()
        for c in range(chips):
            slot = 2 * c + 1 - core
            remote(src, dst.at[slot], ps.at[c], pr.at[c], self.axis, partner).wait_recv()
        for c in range(chips):
            remote(src, dst.at[2 * c + core], ps.at[c], pr.at[c], self.axis, partner).wait_send()
        for k in range(chips - 1):

            @pl.when(jnp.logical_and(chip < chips - 1, k <= chip))
            def _():
                remote(src, dst.at[me], rs.at[k], rr.at[k], self.axis, me + 2).wait_send()

            @pl.when(jnp.logical_and(chip > 0, k <= chips - 1 - chip))
            def _():
                remote(src, dst.at[me], ls.at[k], lr.at[k], self.axis, me - 2).wait_send()

        pltpu.make_async_copy(src, dst.at[me], own).wait()


class Turn:
    axis = "all"

    def __init__(self, array):
        self.array = array

    def plan(self, sizes):
        self.dp, self.n = sizes["dp"], sizes["ctx"]
        self.m = self.n // self.dp
        self.out = jax.ShapeDtypeStruct(self.array.shape, self.array.dtype)
        self.scratch = [pltpu.SemaphoreType.DMA((self.m,))] * 2

    def each(self, src, dst, send, recv):
        row, col = lax.axis_index("dp"), lax.axis_index("ctx")
        put = col % self.m
        for i in range(self.m):
            to_row, to_col = col // self.m, row * self.m + i
            here = jnp.logical_and(to_row == row, to_col == col)
            far = pltpu.make_async_remote_copy(
                src_ref=src.at[i],
                dst_ref=dst.at[put],
                send_sem=send.at[i],
                recv_sem=recv.at[put],
                device_id={"dp": to_row, "ctx": to_col},
                device_id_type=pl.DeviceIdType.MESH,
            )
            local = pltpu.make_async_copy(src.at[i], dst.at[put], recv.at[put])
            yield i, here, far, local

    def start(self, *refs):
        for i, here, far, local in self.each(*refs):
            pl.when(here)(local.start)
            pl.when(jnp.logical_not(here))(far.start)

    def finish(self, src, dst, send, recv):
        row, col = lax.axis_index("dp"), lax.axis_index("ctx")
        for i, here, far, local in self.each(src, dst, send, recv):
            pl.when(jnp.logical_not(here))(far.wait_send)
        for i in range(self.m):
            own = jnp.logical_and(col // self.m == row, row * self.m + i == col)
            local = pltpu.make_async_copy(src.at[i], dst.at[i], recv.at[i])
            far = pltpu.make_async_remote_copy(
                src_ref=src.at[i],
                dst_ref=dst.at[i],
                send_sem=send.at[i],
                recv_sem=recv.at[i],
                device_id={"dp": col // self.m, "ctx": row * self.m + i},
                device_id_type=pl.DeviceIdType.MESH,
            )
            pl.when(own)(local.wait)
            pl.when(jnp.logical_not(own))(far.wait_recv)

    def middle(self, *refs):
        pass


class Swap:
    def __init__(self, axis, array):
        self.axis, self.array = axis, array

    def plan(self, sizes):
        self.n = sizes[self.axis]
        self.out = jax.ShapeDtypeStruct(self.array.shape, self.array.dtype)
        self.scratch = [pltpu.SemaphoreType.DMA((self.n,))] * 2 + [pltpu.SemaphoreType.DMA(())]

    def start(self, src, dst, send, recv, own):
        me = lax.axis_index(self.axis)
        self.local = pltpu.make_async_copy(src.at[me], dst.at[me], own)
        self.local.start()
        self.copies = []
        for k in range(1, self.n):
            peer = lax.rem(me + k, self.n)
            copy = remote(src.at[peer], dst.at[me], send.at[k], recv.at[k], self.axis, peer)
            copy.start()
            self.copies.append(copy)

    def middle(self, *refs):
        pass

    def finish(self, src, dst, send, recv, own):
        me = lax.axis_index(self.axis)
        for k in range(1, self.n):
            slot = lax.rem(me + self.n - k, self.n)
            remote(
                src.at[slot], dst.at[slot], send.at[k], recv.at[k], self.axis, slot
            ).wait_recv()
        for copy in self.copies:
            copy.wait_send()
        self.local.wait()


class Shift:
    def __init__(self, axis, array, by):
        self.axis, self.array, self.by = axis, array, by

    def plan(self, sizes):
        self.n = sizes[self.axis]
        self.out = jax.ShapeDtypeStruct(self.array.shape, self.array.dtype)
        self.scratch = [pltpu.SemaphoreType.DMA(())] * 2

    def start(self, src, dst, send, recv):
        me = lax.axis_index(self.axis)
        peer = lax.rem(me + self.n + self.by, self.n)
        self.copy = remote(src, dst, send, recv, self.axis, peer)
        self.copy.start()

    def middle(self, *refs):
        pass

    def finish(self, *refs):
        self.copy.wait_recv()
        self.copy.wait_send()


class Reduce:
    axis = "ctx"

    def __init__(self, array):
        self.array = array

    def plan(self, sizes):
        self.n = sizes[self.axis]
        block = self.array.shape[1:]
        chips = self.n // 2
        self.out = jax.ShapeDtypeStruct(block, f32)
        slots = pltpu.VMEM((chips,) + block, self.array.dtype)
        self.scratch = [pltpu.SemaphoreType.DMA((chips,))] * 4 + [slots] * 3

    def start(self, src, dst, psend, precv, send, recv, near, term, far):
        me = lax.axis_index(self.axis)
        chips = self.n // 2
        chip, core = me // 2, me % 2
        partner = me + 1 - 2 * core
        self.copies = []
        for k in list(range(1, chips)) + [0]:
            slot = lax.rem(chip + k, chips) * 2 + 1 - core
            copy = remote(
                src.at[slot], near.at[k], psend.at[k], precv.at[k], self.axis, partner
            )
            copy.start()
            self.copies.append(copy)

    def middle(self, src, dst, psend, precv, send, recv, near, term, far):
        me = lax.axis_index(self.axis)
        chips = self.n // 2
        chip, core = me // 2, me % 2
        partner = me + 1 - 2 * core
        for k in range(1, chips):
            remote(
                src.at[me], near.at[k], psend.at[k], precv.at[k], self.axis, partner
            ).wait_recv()
            peer = lax.rem(chip + k, chips) * 2 + core
            both = src[peer].astype(f32) + near[k].astype(f32)
            term[k] = both.astype(term.dtype)
            copy = remote(term.at[k], far.at[k], send.at[k], recv.at[k], self.axis, peer)
            copy.start()
            self.copies.append(copy)

    def finish(self, src, dst, psend, precv, send, recv, near, term, far):
        me = lax.axis_index(self.axis)
        chips = self.n // 2
        core = me % 2
        partner = me + 1 - 2 * core
        remote(src.at[me], near.at[0], psend.at[0], precv.at[0], self.axis, partner).wait_recv()
        dst[...] = src[me].astype(f32) + near[0].astype(f32)
        for k in range(1, chips):
            remote(
                src.at[me], far.at[k], send.at[k], recv.at[k], self.axis, partner
            ).wait_recv()
            dst[...] += far[k].astype(f32)
        for copy in self.copies:
            copy.wait_send()


def exchange(ident, *tasks):
    sizes = {axis: lax.axis_size(axis) for axis in ("dp", "ctx")}
    for task in tasks:
        task.plan(sizes)
    axes = [axis for axis in ("dp", "ctx") if any(task.axis == axis for task in tasks)]
    everyone = any(task.axis == "all" for task in tasks)
    axes = [] if everyone else axes
    count = len(tasks)

    def kernel(*refs):
        barrier = pltpu.get_barrier_semaphore()
        greeted = 0
        if everyone:
            row, col = lax.axis_index("dp"), lax.axis_index("ctx")
            for i in range(1, sizes["dp"] * sizes["ctx"]):
                other = lax.rem(row * sizes["ctx"] + col + i, sizes["dp"] * sizes["ctx"])
                pl.semaphore_signal(
                    barrier,
                    inc=1,
                    device_id={"dp": other // sizes["ctx"], "ctx": other % sizes["ctx"]},
                    device_id_type=pl.DeviceIdType.MESH,
                )
                greeted += 1
        for axis in axes:
            me, n = lax.axis_index(axis), sizes[axis]
            for k in range(1, n):
                pl.semaphore_signal(
                    barrier,
                    inc=1,
                    device_id={axis: lax.rem(me + k, n)},
                    device_id_type=pl.DeviceIdType.MESH,
                )
            greeted += n - 1
        pl.semaphore_wait(barrier, greeted)
        held, at = [], 2 * count
        for i, task in enumerate(tasks):
            held.append((refs[i], refs[count + i]) + tuple(refs[at : at + len(task.scratch)]))
            at += len(task.scratch)
        for task, own in zip(tasks, held):
            task.start(*own)
        for k in range(sizes["ctx"] // 2 - 1):
            for task, own in zip(tasks, held):
                if isinstance(task, Relay):
                    task.step(k, *own)
                elif k == 0:
                    task.middle(*own)
        for task, own in zip(tasks, held):
            task.finish(*own)

    return pl.pallas_call(
        kernel,
        out_shape=[task.out for task in tasks],
        in_specs=[pl.BlockSpec(memory_space=pltpu.VMEM)] * count,
        out_specs=[pl.BlockSpec(memory_space=pltpu.VMEM)] * count,
        scratch_shapes=[shape for task in tasks for shape in task.scratch],
        compiler_params=pltpu.CompilerParams(
            collective_id=ident, has_side_effects=True, vmem_limit_bytes=60 * 1024 * 1024
        ),
        name=f"exchange_{ident}",
    )(*[task.array for task in tasks])


def mm(a, b, dims):
    return lax.dot_general(a, b, ((dims[:1], dims[1:]), ((), ())), preferred_element_type=f32)


def nn(a, b):
    return mm(a, b, (1, 0))


def nt(a, b):
    return mm(a, b, (1, 1))


def tn(a, b):
    return mm(a, b, (0, 0))


def turned(rows):
    width = rows.shape[-1]
    parts = rows.reshape(-1, 2, HEAD_DIM // 2, width)
    return jnp.concatenate([-parts[:, 1:], parts[:, :1]], axis=1).reshape(rows.shape)


def rope_tables(row_count):
    half = HEAD_DIM // 2
    frequency = rope_base ** (-jnp.arange(half).astype(f32) * 2.0 / HEAD_DIM)
    angles = jnp.arange(row_count).astype(f32)[:, None] * frequency[None, :]
    return jnp.tile(jnp.cos(angles), (1, 2)), jnp.tile(jnp.sin(angles), (1, 2))


def norm_backward(hidden, inverse, gain_vec, upstream):
    scaled = upstream * gain_vec
    cubed = inverse * inverse * inverse
    d_hidden = (
        inverse * scaled
        - hidden
        * cubed
        * jnp.sum(scaled * hidden, axis=-1, keepdims=True)
        / hidden.shape[-1]
    )
    return d_hidden, jnp.sum(upstream * hidden * inverse, axis=0)


def inverse_rms(hidden):
    return lax.rsqrt(jnp.mean(hidden * hidden, axis=-1, keepdims=True) + epsilon)


def masked_scores(queries, keys, first):
    scores = nt(queries, keys) * HEAD_DIM ** (-0.5)
    rows = first + lax.broadcasted_iota(jnp.int32, scores.shape, 0)
    return jnp.where(rows >= lax.broadcasted_iota(jnp.int32, scores.shape, 1), scores, -1e30)


def shards(
    inputs, cotangent, w_query, w_key, w_value, w_output, w_gate, w_up, w_down, gain_attn, gain_ffn
):
    dp, ctx = lax.axis_size("dp"), lax.axis_size("ctx")
    me = lax.axis_index("ctx")
    rows, width = inputs.shape
    length = rows * ctx
    q_w, k_w, o_w, f_w = w_query.shape[1], w_key.shape[1], w_output.shape[1], w_gate.shape[1]
    in_rows = w_query.shape[0]
    held = -(-HEADS // ctx)
    wide = held * HEAD_DIM
    total = ctx * wide
    near = all(wide * j >= q_w * j and wide * (j + 1) <= q_w * (j + 2) for j in range(ctx))

    each = ctx // dp
    gains = jnp.stack([gain_attn, gain_ffn])
    kv_rows = jnp.concatenate([w_key, w_value], axis=1).T
    qo_rows = jnp.concatenate([w_query, w_output], axis=1).T
    down_rows = w_down.reshape(each, f_w, o_w).transpose(0, 2, 1)
    kv_rows, all_x, qo_all, all_gains, down_rows = exchange(
        0,
        Relay(kv_rows),
        Relay(inputs),
        Gather(qo_rows),
        Relay(gains),
        Turn(down_rows),
    )
    qo_all = qo_all.transpose(1, 0, 2).reshape(q_w + o_w, width)
    q_part = qo_all[:q_w]
    o_part = jnp.pad(qo_all[q_w:], ((0, 0), (0, total - HEADS * HEAD_DIM)))
    o_part = o_part.reshape(o_w, ctx, wide).transpose(1, 0, 2)

    q_next, o_mine, kv_all, all_cot, down_mine, w_gu = exchange(
        1,
        Shift("ctx", q_part, -1) if near else Relay(q_part),
        Swap("ctx", o_part),
        Gather(kv_rows),
        Relay(cotangent),
        Gather(down_rows),
        Gather(jnp.concatenate([w_gate, w_up], axis=1)),
    )
    w_gu = w_gu.reshape(width, 2 * f_w)
    kv_all = kv_all.transpose(1, 2, 0, 3).reshape(ctx, 2 * k_w, width)
    if near:
        q_rows = jnp.concatenate(
            [q_part, jnp.where(me == ctx - 1, jnp.zeros_like(q_next), q_next)], axis=0
        )
        q_rows = jnp.pad(q_rows, ((0, wide), (0, 0)))
        wq = lax.dynamic_slice(q_rows, (me * (wide - q_w), 0), (wide, width))
    else:
        q_rows = jnp.pad(q_next.reshape(-1, width), ((0, total - HEADS * HEAD_DIM), (0, 0)))
        wq = lax.dynamic_slice(q_rows, (me * wide, 0), (wide, width))
    wk_all = kv_all[:, :k_w].reshape(-1, width)
    wv_all = kv_all[:, k_w:].reshape(-1, width)
    kv_head = [jnp.minimum((me * held + h) // GROUP, KV_HEADS - 1) for h in range(held)]

    def of_heads(array):
        return jnp.concatenate(
            [lax.dynamic_slice(array, (k * HEAD_DIM, 0), (HEAD_DIM, width)) for k in kv_head]
        )

    wk, wv = of_heads(wk_all), of_heads(wv_all)
    wo = o_mine.reshape(ctx * o_w, wide)
    w_down_t = down_mine.reshape(ctx * o_w, f_w)
    gain_rows = all_gains.transpose(1, 0, 2).reshape(2, width).astype(f32)
    gain_one, gain_two = gain_rows[0], gain_rows[1]

    x_full = all_x.reshape(length, width)
    cot_full = all_cot.reshape(length, width)
    hid_full = x_full.astype(f32)
    normed_one = (hid_full * inverse_rms(hid_full) * gain_one).astype(bf16)
    cosine, sine = rope_tables(length)
    cosine, sine = jnp.tile(cosine, (1, held)), jnp.tile(sine, (1, held))
    projected = nt(normed_one, jnp.concatenate([wq, turned(wq), wk, turned(wk), wv]))
    q_a, q_b, k_a, k_b, v_a = [projected[:, i * wide : (i + 1) * wide] for i in range(5)]
    queries = (q_a * cosine + q_b * sine).astype(bf16)
    q_side = (q_a * sine - q_b * cosine).astype(bf16)
    keys = (k_a * cosine + k_b * sine).astype(bf16)
    k_side = (k_a * sine - k_b * cosine).astype(bf16)
    values = v_a.astype(bf16)

    def head(array, h):
        return array[:, h * HEAD_DIM : (h + 1) * HEAD_DIM]

    chunk = min(256, length)
    firsts = list(range(0, length, chunk))
    attended, logsums = [], []
    for h in range(held):
        q_h, k_h, v_h = head(queries, h), head(keys, h), head(values, h)
        outs, logs = [], []
        for first in firsts:
            last = first + chunk
            scores = masked_scores(q_h[first:last], k_h[:last], first)
            top = jnp.max(scores, axis=-1, keepdims=True)
            expo = jnp.exp(scores - top)
            weight = jnp.sum(expo, axis=-1, keepdims=True)
            outs.append(nn(expo.astype(bf16), v_h[:last]) / weight)
            logs.append(top + jnp.log(weight))
        real = me * held + h < HEADS
        attended.append(jnp.where(real, jnp.concatenate(outs), 0.0).astype(bf16))
        logsums.append(logs)
    attended_all = jnp.concatenate(attended, axis=1)

    (mid_sum,) = exchange(2, Reduce(nt(attended_all, wo).astype(bf16).reshape(ctx, rows, width)))
    hidden = inputs.astype(f32)
    middle = hidden + mid_sum
    inv_two = inverse_rms(middle)
    normed_two_mine = (middle * inv_two * gain_two).astype(bf16)
    (normed_two,) = exchange(3, Relay(normed_two_mine))
    normed_two = normed_two.reshape(length, width)

    both = nn(normed_two, w_gu)
    gate_pre, up_pre = both[:, :f_w], both[:, f_w:]
    d_mixed = nn(cot_full, w_down_t)
    sigma = jax.nn.sigmoid(gate_pre)
    silu_gate = gate_pre * sigma
    mixed_act = (silu_gate * up_pre).astype(bf16)
    d_gate = (d_mixed * up_pre * sigma * (1.0 + gate_pre * (1.0 - sigma))).astype(bf16)
    d_up = (d_mixed * silu_gate).astype(bf16)
    d_both = jnp.concatenate([d_gate, d_up], axis=1)
    out_part = nt(mixed_act, w_down_t).astype(bf16)
    d_two_part = nt(d_both, w_gu).astype(bf16)
    g_down = tn(cot_full, mixed_act).astype(bf16)
    g_gu = tn(normed_two, d_both).astype(bf16)

    d_norm_two, g_gu_all = exchange(
        4,
        Reduce(d_two_part.reshape(ctx, rows, width)),
        Swap("dp", g_gu.reshape(dp, in_rows, 2 * f_w)),
    )
    g_gu_sum = jnp.sum(g_gu_all.astype(f32), axis=0)
    d_mid_norm, g_gain_two = norm_backward(middle, inv_two, gain_two, d_norm_two)
    d_middle = cotangent.astype(f32) + d_mid_norm
    d_mid_full, g_down_all, out_sum = exchange(
        5,
        Relay(d_middle.astype(bf16)),
        Swap("dp", g_down.reshape(dp, each, o_w, f_w)),
        Reduce(out_part.reshape(ctx, rows, width)),
    )
    out_act = (middle + out_sum).astype(bf16)
    d_mid_full = d_mid_full.reshape(length, width)
    g_down_part = jnp.sum(g_down_all.astype(f32), axis=0).astype(bf16)

    g_out = tn(d_mid_full, attended_all).astype(bf16)
    d_attended = nn(d_mid_full, wo).astype(bf16)
    dq_all, dk_all, dv_all = [], [], []
    for h in range(held):
        q_h, k_h, v_h = head(queries, h), head(keys, h), head(values, h)
        q_two = jnp.concatenate([q_h, head(q_side, h)], axis=1)
        k_two = jnp.concatenate([k_h, head(k_side, h)], axis=1)
        grad_h = head(d_attended, h)
        delta = jnp.sum(grad_h.astype(f32) * attended[h].astype(f32), axis=-1, keepdims=True)
        dq_parts = []
        dk = jnp.zeros((length, 2 * HEAD_DIM), f32)
        dv = jnp.zeros((length, HEAD_DIM), f32)
        for i, first in enumerate(firsts):
            last = first + chunk
            probs = jnp.exp(masked_scores(q_h[first:last], k_h[:last], first) - logsums[h][i])
            d_probs = nt(grad_h[first:last], v_h[:last])
            d_scores = (probs * (d_probs - delta[first:last])).astype(bf16)
            dq_parts.append(nn(d_scores, k_two[:last]))
            tail = ((0, length - last), (0, 0))
            dk = dk + jnp.pad(tn(d_scores, q_two[first:last]), tail)
            dv = dv + jnp.pad(tn(probs.astype(bf16), grad_h[first:last]), tail)
        dq = jnp.concatenate(dq_parts)
        real = me * held + h < HEADS
        cos_h, sin_h = head(cosine, 0), head(sine, 0)

        def back(two):
            turned_back = two[:, :HEAD_DIM] * cos_h + two[:, HEAD_DIM:] * sin_h
            return jnp.where(real, turned_back * HEAD_DIM ** (-0.5), 0.0).astype(bf16)

        dq_all.append(back(dq))
        dk_all.append(back(dk))
        dv_all.append(jnp.where(real, dv, 0.0).astype(bf16))
    d_qkv = jnp.concatenate(dq_all + dk_all + dv_all, axis=1)
    d_one_f = nn(d_qkv, jnp.concatenate([wq, wk, wv]))
    d_one_part = d_one_f.astype(bf16)
    g_gain_one = jnp.sum(d_one_f * hid_full * inverse_rms(hid_full), axis=0)
    g_gain = jnp.stack([g_gain_one, g_gain_two]).reshape(2, ctx, -1).transpose(1, 0, 2)
    g_qkv = tn(d_qkv, normed_one).astype(bf16)
    g_qkv = g_qkv.reshape(3 * wide, dp, in_rows).transpose(1, 0, 2)

    d_norm_one, g_out_all, g_qkv_all, g_down_mine, gain_all = exchange(
        6,
        Reduce(d_one_part.reshape(ctx, rows, width)),
        Swap("ctx", g_out.reshape(ctx, o_w, wide)),
        Swap("dp", g_qkv),
        Turn(g_down_part),
        Swap("ctx", g_gain),
    )
    inv_one = inverse_rms(hidden)
    d_in_norm, _ = norm_backward(hidden, inv_one, gain_one, d_norm_one)
    grad_input = d_middle + d_in_norm
    g_down_sum = g_down_mine.astype(f32).transpose(0, 2, 1).reshape(each * f_w, o_w)
    g_qkv_sum = jnp.sum(g_qkv_all.astype(f32), axis=0)
    gq_part = g_qkv_sum[:wide].astype(bf16)
    g_kv = jnp.zeros((2, KV_HEADS * HEAD_DIM, in_rows), f32)
    for kind in range(2):
        for h in range(held):
            at = (kind, kv_head[h] * HEAD_DIM, 0)
            base = (1 + kind) * wide + h * HEAD_DIM
            block = lax.dynamic_slice(g_kv, at, (1, HEAD_DIM, in_rows))
            g_kv = lax.dynamic_update_slice(
                g_kv, block + g_qkv_sum[None, base : base + HEAD_DIM], at
            )
    g_kv = g_kv.astype(bf16).reshape(2, ctx, k_w, in_rows).transpose(1, 0, 2, 3)
    g_kv = g_kv.reshape(ctx, 2 * k_w, in_rows)
    g_out_rows = g_out_all.transpose(0, 2, 1).reshape(total, o_w)[: HEADS * HEAD_DIM]
    if near:
        q_task = Shift("ctx", gq_part, 1)
    else:
        q_place = lax.dynamic_update_slice(
            jnp.zeros((total, in_rows), bf16), gq_part, (me * wide, 0)
        )
        q_task = Reduce(q_place[: HEADS * HEAD_DIM].reshape(ctx, q_w, in_rows))
    kv_sum, q_got, g_out_mine, gain_all = exchange(
        7,
        Reduce(g_kv),
        q_task,
        Swap("dp", g_out_rows.reshape(dp, in_rows, o_w)),
        Gather(jnp.sum(gain_all, axis=0)),
    )
    if near:
        q_rows = jnp.concatenate([q_got, gq_part], axis=0)
        g_query = lax.dynamic_slice(
            q_rows, (wide - me * (wide - q_w), 0), (q_w, in_rows)
        ).astype(f32)
    else:
        g_query = q_got
    gain_sum = jnp.sum(gain_all, axis=0)
    return (
        out_act,
        grad_input,
        g_query.T,
        kv_sum[:k_w].T,
        kv_sum[k_w:].T,
        jnp.sum(g_out_mine.astype(f32), axis=0),
        g_gu_sum[:, :f_w],
        g_gu_sum[:, f_w:],
        g_down_sum,
        gain_sum[0],
        gain_sum[1],
    )


def solution(mesh):
    blocks = P(("dp", "ctx"), None)
    matrix = P("dp", "ctx")
    in_specs = (blocks,) * 2 + (matrix,) * 7 + (P("ctx"),) * 2
    return jax.shard_map(shards, mesh=mesh, in_specs=in_specs, out_specs=in_specs, check_vma=False)
```
